512 devices in a mesh: grp: 4 (over y_lo, core), src: 16 (over y_hi, x), rcv: 8 (over z).
Axes of the slice: x: 4, y: 8 (y_hi: 4, y_lo: 2; y = y_hi * 2 + y_lo), z: 8, core: 2. Of those that a mesh axis runs over, the one named last changes fastest.
Arguments:
- recorded: bfloat16 [4, 2, 4096, 4096], P('grp', None, 'src', 'rcv'), parts along dimension 0, as said below
- aperture: int32 [128, 32, 3], P(('grp', 'src'), 'rcv'), parts along dimension 0, may hold values from 0 to 32, as said below
Outputs:
- multiples: float32 [4, 2, 4096, 4096], P('grp', None, 'src', 'rcv'), parts along dimension 0
The draws below stay inside these ranges and needn't reach their ends.
There are 4 independent parts, one for each index of `grp`. The reference program is written for one: setup_inputs(seed, part) draws one part's arguments, and reference() takes and returns one part's arrays. A program takes and returns all parts, laid end to end along the dimension named above; each array names one. Nothing has to cross between parts.
Inputs may be any that keep to these rules, and one draw needn't show every extreme that they name: The data obey reciprocity: recorded(f, c, q, j) equals recorded(f, c, j, q). `aperture`: field 1 is from 4 to 32, field 0 plus field 1 is at most 32, field 2 is from 0 to 2. In every draw some tile pair spans all 32 k-blocks and some has taper width 2.
All inputs are finite; a program needn't handle non-finite values.
Results may differ from the reference program's by a relative error of at most 0.0004.
Values may be sent and summed in bfloat16 or wider, within the bound.
No kernel may reach another device: no remote copies, remote signals or barrier semaphores. Data moves between devices by JAX's collectives and lax.ppermute only.
A program may use at most 64 MiB of HBM per device.

```python
import jax
import jax.numpy as jnp
from jax import lax

NB = 32
TILE = 128
FREQ = 1
LMIN = 4
TAPER_MAX = 2
N = 4096


def draw_recorded(key, part):
    noise = jax.random.normal(key, (FREQ, 2, N, N), jnp.float32)
    noise = jnp.clip(noise, -4.0, 4.0)
    return ((noise + jnp.swapaxes(noise, 2, 3)) * 0.088).astype(jnp.bfloat16)


def draw_aperture(key, part):
    keys = jax.random.split(key, 5)
    extent = jax.random.randint(keys[0], (NB * NB,), LMIN, NB + 1)
    places = jnp.arange(NB * NB, dtype=jnp.int32)
    widest = jax.random.randint(keys[1], (), 0, NB * NB)
    extent = jnp.where(places == widest, NB, extent)
    lowest = jax.random.randint(keys[2], (NB * NB,), 0, NB - extent + 1)
    taper_width = jax.random.randint(keys[3], (NB * NB,), 0, TAPER_MAX + 1)
    steepest = jax.random.randint(keys[4], (), 0, NB * NB)
    taper_width = jnp.where(places == steepest, TAPER_MAX, taper_width)
    fields = jnp.stack([lowest, extent, taper_width], axis=-1)
    return fields.reshape(NB, NB, 3).astype(jnp.int32)


def setup_inputs(seed: int = 0, part: int = 0) -> dict:
    splits = jax.random.split(jax.random.key(seed), 3)
    part_keys = jax.random.split(jax.random.fold_in(splits[2], part), 3)
    return {
        "recorded": draw_recorded(jax.random.fold_in(jax.random.fold_in(splits[2], part), 71), part),
        "aperture": draw_aperture(jax.random.fold_in(jax.random.fold_in(splits[2], part), 71), part),
    }


def tile_weights(aperture):
    block_ids = jnp.arange(NB, dtype=jnp.int32)
    offset = block_ids[None, None, :] - aperture[..., 0:1]
    extent = aperture[..., 1:2]
    taper_width = aperture[..., 2:3]
    margin = jnp.minimum(offset, extent - 1 - offset)
    ramped = jnp.minimum(1.0, (margin + 1).astype(jnp.float32) / (taper_width + 1).astype(jnp.float32))
    return jnp.where((offset >= 0) & (offset < extent), ramped, 0.0).astype(jnp.float32)


def reference(recorded, aperture):
    weights = tile_weights(aperture)
    right_side = recorded.astype(jnp.float32).reshape(FREQ, 2, N, NB, TILE)

    def source_row(tile_index):
        panel = lax.dynamic_slice_in_dim(recorded, tile_index * TILE, TILE, 2)
        row_weight = jnp.repeat(lax.dynamic_index_in_dim(weights, tile_index, 0, keepdims=False), TILE, axis=1)
        scaled = (panel[:, :, None, :, :].astype(jnp.float32) * row_weight[None, None, :, None, :]).astype(jnp.bfloat16)
        products = jnp.einsum("fatik,fbktj->fabtij", scaled.astype(jnp.float32), right_side, precision=lax.Precision.HIGHEST)
        real_part = products[:, 0, 0] - products[:, 1, 1]
        imag_part = products[:, 0, 1] + products[:, 1, 0]
        stacked = jnp.stack([real_part, imag_part], 1)
        return stacked.transpose(0, 1, 3, 2, 4).reshape(FREQ, 2, TILE, N)

    stacked_rows = lax.map(source_row, jnp.arange(NB, dtype=jnp.int32))
    return stacked_rows.transpose(1, 2, 0, 3, 4).reshape(FREQ, 2, N, N)
```

```python
import functools

import jax
import jax.numpy as jnp
from jax import lax
from jax.experimental import pallas as pl
from jax.experimental.pallas import tpu as pltpu
from jax.sharding import PartitionSpec as P

NB = 32
TILE = 128
GRID_Y = 4
GRID_X = 4
ROWS = 256
COLS = 512


def tile_weights(aperture):
    block_ids = jnp.arange(NB, dtype=jnp.int32)
    offset = block_ids[None, None, :] - aperture[..., 0:1]
    extent = aperture[..., 1:2]
    taper_width = aperture[..., 2:3]
    margin = jnp.minimum(offset, extent - 1 - offset)
    ramped = jnp.minimum(
        1.0, (margin + 1).astype(jnp.float32) / (taper_width + 1).astype(jnp.float32)
    )
    return jnp.where((offset >= 0) & (offset < extent), ramped, 0.0)


def shift(block, dy, dx):
    pairs = [
        (GRID_X * y + x, GRID_X * ((y + dy) % GRID_Y) + (x + dx) % GRID_X)
        for y in range(GRID_Y)
        for x in range(GRID_X)
    ]
    return lax.ppermute(block, "src", pairs)


def accumulate(has_base, pieces, weights, places, left, *refs):
    if has_base:
        base, refs = refs[0], refs[1:]
    blocks, out = refs[:pieces], refs[pieces]
    for tile in range(COLS // TILE):
        cols = slice(tile * TILE, (tile + 1) * TILE)
        total = None
        for number in range(pieces):
            place = places[number]
            start = pl.multiple_of(place * ROWS, ROWS)
            parts = []
            for half in range(ROWS // TILE):
                lanes = pl.ds(pl.multiple_of(start + half * TILE, TILE), TILE)
                rows = []
                for part in range(2):
                    for a in range(2):
                        value = left[0, part, a * TILE : (a + 1) * TILE, lanes]
                        weight = weights[a * 4 + tile, 2 * place + half]
                        rows.append((value.astype(jnp.float32) * weight).astype(jnp.bfloat16))
                parts.append(jnp.concatenate(rows, axis=0))
            scaled = jnp.concatenate(parts, axis=1)
            block = blocks[number]
            right = jnp.concatenate([block[0, 0, :, cols], block[0, 1, :, cols]], axis=1)
            product = jnp.dot(scaled, right, preferred_element_type=jnp.float32)
            total = product if total is None else total + product
        real = total[:ROWS, :TILE] - total[ROWS:, TILE:]
        imag = total[:ROWS, TILE:] + total[ROWS:, :TILE]
        if has_base:
            real = real + base[0, 0, :, cols]
            imag = imag + base[0, 1, :, cols]
        out[0, 0, :, cols] = real
        out[0, 1, :, cols] = imag


def add_blocks(weights, places, left, blocks, base=None):
    count = len(blocks)
    smem = pl.BlockSpec(memory_space=pltpu.SMEM)
    vmem = pl.BlockSpec(memory_space=pltpu.VMEM)
    extra = () if base is None else (base,)
    return pl.pallas_call(
        functools.partial(accumulate, base is not None, count),
        out_shape=jax.ShapeDtypeStruct((1, 2, ROWS, COLS), jnp.float32),
        in_specs=[smem, smem] + [vmem] * (1 + len(extra) + count),
        out_specs=vmem,
        compiler_params=pltpu.CompilerParams(vmem_limit_bytes=40 << 20),
        cost_estimate=pl.CostEstimate(
            flops=count * 2 * 4 * ROWS * ROWS * COLS,
            bytes_accessed=count * (1 << 19) + (5 << 20),
            transcendentals=0,
        ),
    )(weights, places, left, *extra, *blocks)


def shards(recorded, aperture):
    weights = tile_weights(aperture).reshape(8, NB)
    own = recorded
    left = lax.all_gather(recorded, "rcv", axis=3, tiled=True)
    got = {(0, 0): own}
    got[1, 0] = shift(own, 1, 0)
    got[3, 0] = shift(own, -1, 0)
    got[0, 1] = shift(own, 0, 1)
    got[0, 3] = shift(own, 0, -1)
    far = [shift(got[0, 1][:, :1], 0, 1), shift(got[0, 3][:, 1:], 0, -1)]
    got[0, 2] = jnp.concatenate(far, axis=1)
    far = [shift(got[1, 0][:, :1], 1, 0), shift(got[3, 0][:, 1:], -1, 0)]
    got[2, 0] = jnp.concatenate(far, axis=1)
    for row in (1, 3):
        got[row, 1] = shift(got[row, 0], 0, 1)
        got[row, 3] = shift(got[row, 0], 0, -1)
    got[1, 2] = shift(got[0, 2], 1, 0)
    got[3, 2] = shift(got[0, 2], -1, 0)
    got[2, 1] = shift(got[2, 0], 0, 1)
    got[2, 3] = shift(got[2, 0], 0, -1)
    far = [shift(got[2, 1][:, :1], 0, 1), shift(got[2, 3][:, 1:], 0, -1)]
    got[2, 2] = jnp.concatenate(far, axis=1)

    source = lax.axis_index("src")
    y, x = source // GRID_X, source % GRID_X

    def places(keys):
        return jnp.stack([(y - dy) % GRID_Y * GRID_X + (x - dx) % GRID_X for dy, dx in keys])

    early = [(0, 0), (1, 0), (3, 0), (0, 1), (0, 3), (0, 2), (2, 0), (1, 1), (1, 3), (3, 1), (3, 3)]
    late = [(1, 2), (3, 2), (2, 1), (2, 3), (2, 2)]
    total = add_blocks(weights, places(early), left, [got[k] for k in early])
    return add_blocks(weights, places(late), left, [got[k] for k in late], total)


def solution(mesh):
    in_specs = (P("grp", None, "src", "rcv"), P(("grp", "src"), "rcv", None))
    out_specs = P("grp", None, "src", "rcv")
    return jax.shard_map(shards, mesh=mesh, in_specs=in_specs, out_specs=out_specs, check_vma=False)
```

```python
import functools

import jax
import jax.numpy as jnp
from jax import lax
from jax.experimental import pallas as pl
from jax.experimental.pallas import tpu as pltpu
from jax.sharding import PartitionSpec as P

NB = 32
TILE = 128
SIDE = 4
ROWS = 256
COLS = 512
X_LINES = [[SIDE * y + x for x in range(SIDE)] for y in range(SIDE)]
Y_LINES = [[SIDE * y + x for y in range(SIDE)] for x in range(SIDE)]


def tile_weights(aperture):
    block_ids = jnp.arange(NB, dtype=jnp.int32)
    offset = block_ids[None, None, :] - aperture[..., 0:1]
    extent = aperture[..., 1:2]
    taper_width = aperture[..., 2:3]
    margin = jnp.minimum(offset, extent - 1 - offset)
    ramped = jnp.minimum(
        1.0, (margin + 1).astype(jnp.float32) / (taper_width + 1).astype(jnp.float32)
    )
    return jnp.where((offset >= 0) & (offset < extent), ramped, 0.0)


def shift(block, dy, dx):
    pairs = [
        (SIDE * y + x, SIDE * ((y + dy) % SIDE) + (x + dx) % SIDE)
        for y in range(SIDE)
        for x in range(SIDE)
    ]
    return lax.ppermute(block, "src", pairs)


def along(block, lines):
    copies = jnp.broadcast_to(block, (SIDE, *block.shape[1:]))
    return lax.all_to_all(copies, "src", 0, 0, tiled=True, axis_index_groups=lines)


def accumulate(steps, has_base, weights, source, left, *refs):
    out, base = refs[-1], refs[-2]
    y, x = source[0] // SIDE, lax.rem(source[0], SIDE)
    terms = []
    for array, index, dy, dx in steps:
        row, column = lax.rem(y + dy, SIDE), lax.rem(x + dx, SIDE)
        index = {"y": row, "x": column}.get(index, index)
        terms.append((row * SIDE + column, refs[array], index))
    for tile in range(COLS // TILE):
        cols = slice(tile * TILE, (tile + 1) * TILE)
        total = None
        for place, block, index in terms:
            parts = []
            for half in range(ROWS // TILE):
                lanes = pl.ds(pl.multiple_of(place * ROWS + half * TILE, TILE), TILE)
                rows = []
                for part in range(2):
                    for a in range(2):
                        value = left[0, part, a * TILE : (a + 1) * TILE, lanes]
                        weight = weights[a * 4 + tile, 2 * place + half]
                        rows.append((value.astype(jnp.float32) * weight).astype(jnp.bfloat16))
                parts.append(jnp.concatenate(rows, axis=0))
            scaled = jnp.concatenate(parts, axis=1)
            right = jnp.concatenate([block[index, 0, :, cols], block[index, 1, :, cols]], axis=1)
            product = jnp.dot(scaled, right, preferred_element_type=jnp.float32)
            total = product if total is None else total + product
        real = total[:ROWS, :TILE] - total[ROWS:, TILE:]
        imag = total[:ROWS, TILE:] + total[ROWS:, :TILE]
        if has_base:
            real, imag = real + base[0, 0, :, cols], imag + base[0, 1, :, cols]
        out[0, 0, :, cols] = real
        out[0, 1, :, cols] = imag


def add_blocks(weights, source, left, arrays, steps, base=None):
    extra = [] if base is None else [base]
    smem = pl.BlockSpec(memory_space=pltpu.SMEM)
    vmem = pl.BlockSpec(memory_space=pltpu.VMEM)
    return pl.pallas_call(
        functools.partial(accumulate, steps, base is not None),
        out_shape=jax.ShapeDtypeStruct((1, 2, ROWS, COLS), jnp.float32),
        in_specs=[smem, smem] + [vmem] * (1 + len(arrays) + len(extra)),
        out_specs=vmem,
        compiler_params=pltpu.CompilerParams(vmem_limit_bytes=20 << 20),
        cost_estimate=pl.CostEstimate(
            flops=len(steps) * 6 * 4 * ROWS * ROWS * COLS,
            bytes_accessed=len(steps) * (1 << 19) + (5 << 20),
            transcendentals=0,
        ),
    )(weights, source, left, *arrays, *extra)


def shards(recorded, aperture):
    weights = tile_weights(aperture).reshape(8, NB)
    source = lax.axis_index("src")
    x = source % SIDE
    y = source // SIDE
    left = lax.all_gather(recorded, "rcv", axis=3, tiled=True)
    above, below = shift(recorded, 1, 0), shift(recorded, -1, 0)
    before, after = shift(recorded, 0, 1), shift(recorded, 0, -1)
    opposite = shift(recorded, 0, 2)
    across = [shift(above[:, :1], 1, 0), shift(below[:, 1:], -1, 0)]
    *across, before, after, opposite = lax.optimization_barrier((*across, before, after, opposite))
    pair = jnp.concatenate([above, below], axis=0)
    pair_left, pair_right = shift(pair, 0, 1), shift(pair, 0, -1)
    across_line = along(jnp.concatenate(across, axis=1), X_LINES)
    opposite_above, opposite_below = shift(opposite, 1, 0), shift(opposite, -1, 0)

    early = [recorded, above, below, before, after, opposite, pair_left, pair_right]
    steps = [(0, 0, 0, 0), (1, 0, 3, 0), (2, 0, 1, 0), (3, 0, 0, 3), (4, 0, 0, 1), (5, 0, 0, 2)]
    steps += [(6, 0, 3, 3), (6, 1, 1, 3), (7, 0, 3, 1), (7, 1, 1, 1)]
    source = source.reshape(1)
    total = add_blocks(weights, source, left, early, steps)
    late = [opposite_above, opposite_below, across_line]
    steps = [(0, 0, 3, 2), (1, 0, 1, 2)] + [(2, "x", 2, i) for i in range(SIDE)]
    return add_blocks(weights, source, left, late, steps, total)


def solution(mesh):
    in_specs = (P("grp", None, "src", "rcv"), P(("grp", "src"), "rcv", None))
    out_specs = P("grp", None, "src", "rcv")
    return jax.shard_map(shards, mesh=mesh, in_specs=in_specs, out_specs=out_specs, check_vma=False)
```

```python
import functools

import jax
import jax.numpy as jnp
from jax import lax
from jax.experimental import pallas as pl
from jax.experimental.pallas import tpu as pltpu
from jax.sharding import PartitionSpec as P

NB = 32
TILE = 128
SIDE = 4
ROWS = 256
COLS = 512
X_LINES = [[SIDE * y + x for x in range(SIDE)] for y in range(SIDE)]
Y_LINES = [[SIDE * y + x for y in range(SIDE)] for x in range(SIDE)]


def tile_weights(aperture):
    block_ids = jnp.arange(NB, dtype=jnp.int32)
    offset = block_ids[None, None, :] - aperture[..., 0:1]
    extent = aperture[..., 1:2]
    taper_width = aperture[..., 2:3]
    margin = jnp.minimum(offset, extent - 1 - offset)
    ramped = jnp.minimum(
        1.0, (margin + 1).astype(jnp.float32) / (taper_width + 1).astype(jnp.float32)
    )
    return jnp.where((offset >= 0) & (offset < extent), ramped, 0.0)


def shift(block, dy, dx):
    pairs = [
        (SIDE * y + x, SIDE * ((y + dy) % SIDE) + (x + dx) % SIDE)
        for y in range(SIDE)
        for x in range(SIDE)
    ]
    return lax.ppermute(block, "src", pairs)


def along(block, lines):
    copies = jnp.broadcast_to(block, (SIDE, *block.shape[1:]))
    return lax.all_to_all(copies, "src", 0, 0, tiled=True, axis_index_groups=lines)


def locate(source, steps):
    y, x = source[0] // SIDE, lax.rem(source[0], SIDE)
    found = []
    for _, index, dy, dx in steps:
        row, column = lax.rem(y + dy, SIDE), lax.rem(x + dx, SIDE)
        found.append((row * SIDE + column, {"y": row, "x": column}.get(index, index)))
    return found


def sum_tile(weights, tile, places, lefts, rights):
    cols = slice(tile * TILE, (tile + 1) * TILE)
    total = None
    for place, left, right in zip(places, lefts, rights):
        parts = []
        for half in range(ROWS // TILE):
            lanes = slice(half * TILE, (half + 1) * TILE)
            rows = []
            for part in range(2):
                for a in range(2):
                    value = left[part, a * TILE : (a + 1) * TILE, lanes]
                    weight = weights[a * 4 + tile, 2 * place + half]
                    rows.append((value.astype(jnp.float32) * weight).astype(jnp.bfloat16))
            parts.append(jnp.concatenate(rows, axis=0))
        scaled = jnp.concatenate(parts, axis=1)
        both = jnp.concatenate([right[0, :, cols], right[1, :, cols]], axis=1)
        product = jnp.dot(scaled, both, preferred_element_type=jnp.float32)
        total = product if total is None else total + product
    real = total[:ROWS, :TILE] - total[ROWS:, TILE:]
    imag = total[:ROWS, TILE:] + total[ROWS:, :TILE]
    return cols, real, imag


def sum_early(steps, late, group, weights, source, left, *refs):
    *arrays, out, late_left, lefts, rights, left_done, right_done, late_done = refs

    def columns(place):
        return left.at[0, :, :, pl.ds(pl.multiple_of(place * ROWS, ROWS), ROWS)]

    places, copies = [], []
    for number, (place, index) in enumerate(locate(source, steps)):
        block = arrays[steps[number][0]].at[index]
        pair = (
            pltpu.make_async_copy(columns(place), lefts.at[number], left_done.at[number]),
            pltpu.make_async_copy(block, rights.at[number], right_done.at[number]),
        )
        for copy in pair:
            copy.start()
        places.append(place)
        copies.append(pair)
    kept = [
        pltpu.make_async_copy(columns(place), late_left.at[number], late_done.at[number])
        for number, (place, _) in enumerate(locate(source, late))
    ]
    for copy in kept:
        copy.start()
    for first in range(0, len(steps), group):
        numbers = range(first, min(first + group, len(steps)))
        for number in numbers:
            for copy in copies[number]:
                copy.wait()
        for tile in range(COLS // TILE):
            cols, real, imag = sum_tile(
                weights,
                tile,
                [places[n] for n in numbers],
                [lefts.at[n] for n in numbers],
                [rights.at[n] for n in numbers],
            )
            if first > 0:
                real, imag = real + out[0, 0, :, cols], imag + out[0, 1, :, cols]
            out[0, 0, :, cols] = real
            out[0, 1, :, cols] = imag
    for copy in kept:
        copy.wait()


def sum_late(steps, group, weights, source, base, late_left, *refs):
    *arrays, out, sum_before, lefts, rights, base_done, left_done, right_done = refs
    places, copies = [], []
    for number, (place, index) in enumerate(locate(source, steps)):
        block = arrays[steps[number][0]].at[index]
        pair = (
            pltpu.make_async_copy(late_left.at[number], lefts.at[number], left_done.at[number]),
            pltpu.make_async_copy(block, rights.at[number], right_done.at[number]),
        )
        for copy in pair:
            copy.start()
        places.append(place)
        copies.append(pair)
    fetch = pltpu.make_async_copy(base, sum_before, base_done)
    fetch.start()
    for first in range(0, len(steps), group):
        numbers = range(first, min(first + group, len(steps)))
        for number in numbers:
            for copy in copies[number]:
                copy.wait()
        for tile in range(COLS // TILE):
            cols, real, imag = sum_tile(
                weights,
                tile,
                [places[n] for n in numbers],
                [lefts.at[n] for n in numbers],
                [rights.at[n] for n in numbers],
            )
            if first == 0 and tile == 0:
                fetch.wait()
            before = sum_before if first == 0 else out
            out[0, 0, :, cols] = before[0, 0, :, cols] + real
            out[0, 1, :, cols] = before[0, 1, :, cols] + imag


def cost(count, scale):
    return pl.CostEstimate(
        flops=count * 8 * scale * ROWS * ROWS * COLS,
        bytes_accessed=count * 3 * (1 << 18) + (2 << 20),
        transcendentals=0,
    )


SMEM = pl.BlockSpec(memory_space=pltpu.SMEM)
VMEM = pl.BlockSpec(memory_space=pltpu.VMEM)
HBM = pl.BlockSpec(memory_space=pltpu.HBM)
SUM = jax.ShapeDtypeStruct((1, 2, ROWS, COLS), jnp.float32)


def add_early(weights, source, left, arrays, steps, late):
    count = len(steps)
    return pl.pallas_call(
        functools.partial(sum_early, steps, late, 6),
        out_shape=(SUM, jax.ShapeDtypeStruct((len(late), 2, ROWS, ROWS), jnp.bfloat16)),
        in_specs=[SMEM, SMEM, HBM] + [HBM] * len(arrays),
        out_specs=(VMEM, VMEM),
        scratch_shapes=[
            pltpu.VMEM((count, 2, ROWS, ROWS), jnp.bfloat16),
            pltpu.VMEM((count, 2, ROWS, COLS), jnp.bfloat16),
            pltpu.SemaphoreType.DMA((count,)),
            pltpu.SemaphoreType.DMA((count,)),
            pltpu.SemaphoreType.DMA((len(late),)),
        ],
        compiler_params=pltpu.CompilerParams(vmem_limit_bytes=63 << 20),
        cost_estimate=cost(count, 3),
    )(weights, source, left, *arrays)


def add_late(weights, source, base, late_left, arrays, steps):
    count = len(steps)
    return pl.pallas_call(
        functools.partial(sum_late, steps, 5),
        out_shape=SUM,
        in_specs=[SMEM, SMEM, HBM, HBM] + [HBM] * len(arrays),
        out_specs=VMEM,
        scratch_shapes=[
            pltpu.VMEM((1, 2, ROWS, COLS), jnp.float32),
            pltpu.VMEM((count, 2, ROWS, ROWS), jnp.bfloat16),
            pltpu.VMEM((count, 2, ROWS, COLS), jnp.bfloat16),
            pltpu.SemaphoreType.DMA,
            pltpu.SemaphoreType.DMA((count,)),
            pltpu.SemaphoreType.DMA((count,)),
        ],
        compiler_params=pltpu.CompilerParams(vmem_limit_bytes=60 << 20),
        cost_estimate=cost(count, 3),
    )(weights, source, base, late_left, *arrays)


def shards(recorded, aperture):
    weights = tile_weights(aperture).reshape(8, NB)
    source = lax.axis_index("src")
    x = source % SIDE
    y = source // SIDE
    left = lax.all_gather(recorded, "rcv", axis=3, tiled=True)
    above, below = shift(recorded, 1, 0), shift(recorded, -1, 0)
    before, after = shift(recorded, 0, 1), shift(recorded, 0, -1)
    opposite = shift(recorded, 0, 2)
    across = [shift(above[:, :1], 1, 0), shift(below[:, 1:], -1, 0)]
    *across, before, after, opposite = lax.optimization_barrier((*across, before, after, opposite))
    pair = jnp.concatenate([above, below], axis=0)
    pair_left, pair_right = shift(pair, 0, 1), shift(pair, 0, -1)
    far = jnp.concatenate(across, axis=1)
    across_line = along(far, X_LINES)
    opposite_above, opposite_below = shift(opposite, 1, 0), shift(opposite, -1, 0)

    early = [recorded, above, below, before, after, opposite, pair_left, pair_right, far]
    steps = [(0, 0, 0, 0), (1, 0, 3, 0), (2, 0, 1, 0), (3, 0, 0, 3), (4, 0, 0, 1), (5, 0, 0, 2)]
    steps += [(6, 0, 3, 3), (6, 1, 1, 3), (7, 0, 3, 1), (7, 1, 1, 1)]
    steps += [(8, 0, 2, 0)]
    late = [opposite_above, opposite_below, across_line]
    late_steps = [(0, 0, 3, 2), (1, 0, 1, 2)] + [(2, "x", 2, i) for i in range(1, SIDE)]
    source = source.reshape(1)
    total, late_left = add_early(weights, source, left, early, steps, late_steps)
    return add_late(weights, source, total, late_left, late, late_steps)


def solution(mesh):
    in_specs = (P("grp", None, "src", "rcv"), P(("grp", "src"), "rcv", None))
    out_specs = P("grp", None, "src", "rcv")
    return jax.shard_map(shards, mesh=mesh, in_specs=in_specs, out_specs=out_specs, check_vma=False)
```

```python
import functools

import jax
import jax.numpy as jnp
from jax import lax
from jax.experimental import pallas as pl
from jax.experimental.pallas import tpu as pltpu
from jax.sharding import PartitionSpec as P

NB = 32
TILE = 128
SIDE = 4
ROWS = 256
COLS = 512
X_LINES = [[SIDE * y + x for x in range(SIDE)] for y in range(SIDE)]
Y_LINES = [[SIDE * y + x for y in range(SIDE)] for x in range(SIDE)]


def tile_weights(aperture):
    block_ids = jnp.arange(NB, dtype=jnp.int32)
    offset = block_ids[None, None, :] - aperture[..., 0:1]
    extent = aperture[..., 1:2]
    taper_width = aperture[..., 2:3]
    margin = jnp.minimum(offset, extent - 1 - offset)
    ramped = jnp.minimum(
        1.0, (margin + 1).astype(jnp.float32) / (taper_width + 1).astype(jnp.float32)
    )
    return jnp.where((offset >= 0) & (offset < extent), ramped, 0.0)


def shift(block, dy, dx):
    pairs = [
        (SIDE * y + x, SIDE * ((y + dy) % SIDE) + (x + dx) % SIDE)
        for y in range(SIDE)
        for x in range(SIDE)
    ]
    return lax.ppermute(block, "src", pairs)


def along(block, lines):
    copies = jnp.broadcast_to(block, (SIDE, *block.shape[1:]))
    return lax.all_to_all(copies, "src", 0, 0, tiled=True, axis_index_groups=lines)


def locate(source, steps):
    y, x = source[0] // SIDE, lax.rem(source[0], SIDE)
    found = []
    for _, index, dy, dx in steps:
        row, column = lax.rem(y + dy, SIDE), lax.rem(x + dx, SIDE)
        found.append((row * SIDE + column, {"y": row, "x": column}.get(index, index)))
    return found


def sum_tile(weights, tile, places, lefts, rights):
    cols = slice(tile * TILE, (tile + 1) * TILE)
    total = None
    for place, left, right in zip(places, lefts, rights):
        parts = []
        for half in range(ROWS // TILE):
            lanes = slice(half * TILE, (half + 1) * TILE)
            rows = []
            for part in range(2):
                for a in range(2):
                    value = left[part, a * TILE : (a + 1) * TILE, lanes]
                    weight = weights[a * 4 + tile, 2 * place + half]
                    rows.append((value.astype(jnp.float32) * weight).astype(jnp.bfloat16))
            parts.append(jnp.concatenate(rows, axis=0))
        scaled = jnp.concatenate(parts, axis=1)
        both = jnp.concatenate([right[0, :, cols], right[1, :, cols]], axis=1)
        product = jnp.dot(scaled, both, preferred_element_type=jnp.float32)
        total = product if total is None else total + product
    real = total[:ROWS, :TILE] - total[ROWS:, TILE:]
    imag = total[:ROWS, TILE:] + total[ROWS:, :TILE]
    return cols, real, imag


def sum_early(steps, late, group, weights, source, left, *refs):
    *arrays, out, late_left, lefts, rights, left_done, right_done, late_done = refs

    def columns(place):
        return left.at[0, :, :, pl.ds(pl.multiple_of(place * ROWS, ROWS), ROWS)]

    places, copies = [], []
    for number, (place, index) in enumerate(locate(source, steps)):
        block = arrays[steps[number][0]].at[index]
        pair = (
            pltpu.make_async_copy(columns(place), lefts.at[number], left_done.at[number]),
            pltpu.make_async_copy(block, rights.at[number], right_done.at[number]),
        )
        for copy in pair:
            copy.start()
        places.append(place)
        copies.append(pair)
    kept = [
        pltpu.make_async_copy(columns(place), late_left.at[number], late_done.at[number])
        for number, (place, _) in enumerate(locate(source, late))
    ]
    for copy in kept:
        copy.start()
    for first in range(0, len(steps), group):
        numbers = range(first, min(first + group, len(steps)))
        for number in numbers:
            for copy in copies[number]:
                copy.wait()
        for tile in range(COLS // TILE):
            cols, real, imag = sum_tile(
                weights,
                tile,
                [places[n] for n in numbers],
                [lefts.at[n] for n in numbers],
                [rights.at[n] for n in numbers],
            )
            if first > 0:
                real, imag = real + out[0, 0, :, cols], imag + out[0, 1, :, cols]
            out[0, 0, :, cols] = real
            out[0, 1, :, cols] = imag
    for copy in kept:
        copy.wait()


def sum_late(steps, group, weights, source, base, late_left, *refs):
    *arrays, out, total, partial, lefts, rights, left_done, right_done, base_done, out_done = refs
    places, copies = [], []
    for number, (place, index) in enumerate(locate(source, steps)):
        block = arrays[steps[number][0]].at[index]
        pair = (
            pltpu.make_async_copy(late_left.at[number], lefts.at[number], left_done.at[number]),
            pltpu.make_async_copy(block, rights.at[number], right_done.at[number]),
        )
        for copy in pair:
            copy.start()
        places.append(place)
        copies.append(pair)
    fetch = pltpu.make_async_copy(base, total, base_done)
    fetch.start()
    stores = []
    for first in range(0, len(steps), group):
        numbers = range(first, min(first + group, len(steps)))
        for number in numbers:
            for copy in copies[number]:
                copy.wait()
        last = first + group >= len(steps)
        for tile in range(COLS // TILE):
            cols, real, imag = sum_tile(
                weights,
                tile,
                [places[n] for n in numbers],
                [lefts.at[n] for n in numbers],
                [rights.at[n] for n in numbers],
            )
            if last and first > 0 and tile == 0:
                fetch.wait()
            if first > 0:
                real, imag = real + partial[0, :, cols], imag + partial[1, :, cols]
            if last:
                total[0, 0, :, cols] += real
                total[0, 1, :, cols] += imag
            else:
                partial[0, :, cols] = real
                partial[1, :, cols] = imag
            if last:
                store = pltpu.make_async_copy(
                    total.at[0, :, :, cols], out.at[0, :, :, cols], out_done.at[tile]
                )
                store.start()
                stores.append(store)
    for store in stores:
        store.wait()


def cost(count, scale):
    return pl.CostEstimate(
        flops=count * 8 * scale * ROWS * ROWS * COLS,
        bytes_accessed=count * 3 * (1 << 18) + (2 << 20),
        transcendentals=0,
    )


SMEM = pl.BlockSpec(memory_space=pltpu.SMEM)
VMEM = pl.BlockSpec(memory_space=pltpu.VMEM)
HBM = pl.BlockSpec(memory_space=pltpu.HBM)
SUM = jax.ShapeDtypeStruct((1, 2, ROWS, COLS), jnp.float32)


def add_early(weights, source, left, arrays, steps, late):
    count = len(steps)
    return pl.pallas_call(
        functools.partial(sum_early, steps, late, 6),
        out_shape=(SUM, jax.ShapeDtypeStruct((len(late), 2, ROWS, ROWS), jnp.bfloat16)),
        in_specs=[SMEM, SMEM, HBM] + [HBM] * len(arrays),
        out_specs=(VMEM, VMEM),
        scratch_shapes=[
            pltpu.VMEM((count, 2, ROWS, ROWS), jnp.bfloat16),
            pltpu.VMEM((count, 2, ROWS, COLS), jnp.bfloat16),
            pltpu.SemaphoreType.DMA((count,)),
            pltpu.SemaphoreType.DMA((count,)),
            pltpu.SemaphoreType.DMA((len(late),)),
        ],
        compiler_params=pltpu.CompilerParams(vmem_limit_bytes=63 << 20),
        cost_estimate=cost(count, 3),
    )(weights, source, left, *arrays)


def add_late(weights, source, base, late_left, arrays, steps):
    count = len(steps)
    return pl.pallas_call(
        functools.partial(sum_late, steps, 2),
        out_shape=SUM,
        in_specs=[SMEM, SMEM, HBM, HBM] + [HBM] * len(arrays),
        out_specs=HBM,
        scratch_shapes=[
            pltpu.VMEM((1, 2, ROWS, COLS), jnp.float32),
            pltpu.VMEM((2, ROWS, COLS), jnp.float32),
            pltpu.VMEM((count, 2, ROWS, ROWS), jnp.bfloat16),
            pltpu.VMEM((count, 2, ROWS, COLS), jnp.bfloat16),
            pltpu.SemaphoreType.DMA((count,)),
            pltpu.SemaphoreType.DMA((count,)),
            pltpu.SemaphoreType.DMA,
            pltpu.SemaphoreType.DMA((COLS // TILE,)),
        ],
        compiler_params=pltpu.CompilerParams(vmem_limit_bytes=60 << 20),
        cost_estimate=cost(count, 3),
    )(weights, source, base, late_left, *arrays)


def shards(recorded, aperture):
    weights = tile_weights(aperture).reshape(8, NB)
    source = lax.axis_index("src")
    x = source % SIDE
    y = source // SIDE
    left = lax.all_gather(recorded, "rcv", axis=3, tiled=True)
    above, below = shift(recorded, 1, 0), shift(recorded, -1, 0)
    before, after = shift(recorded, 0, 1), shift(recorded, 0, -1)
    opposite = shift(recorded, 0, 2)
    across = [shift(above[:, :1], 1, 0), shift(below[:, 1:], -1, 0)]
    *across, before, after, opposite, weights = lax.optimization_barrier(
        (*across, before, after, opposite, weights)
    )
    pair = jnp.concatenate([above, below], axis=0)
    pair_left, pair_right = shift(pair, 0, 1), shift(pair, 0, -1)
    far = jnp.concatenate(across, axis=1)
    across_line = along(far, X_LINES)
    opposite_above, opposite_below = shift(opposite, 1, 0), shift(opposite, -1, 0)

    early = [recorded, above, below, before, after, opposite, pair_left, pair_right, far]
    steps = [(0, 0, 0, 0), (1, 0, 3, 0), (2, 0, 1, 0), (3, 0, 0, 3), (4, 0, 0, 1), (5, 0, 0, 2)]
    steps += [(6, 0, 3, 3), (6, 1, 1, 3), (7, 0, 3, 1), (7, 1, 1, 1)]
    steps += [(8, 0, 2, 0)]
    late = [opposite_above, opposite_below, across_line]
    late_steps = [(0, 0, 3, 2), (1, 0, 1, 2)] + [(2, "x", 2, i) for i in range(1, SIDE)]
    source = source.reshape(1)
    total, late_left = add_early(weights, source, left, early, steps, late_steps)
    return add_late(weights, source, total, late_left, late, late_steps)


def solution(mesh):
    in_specs = (P("grp", None, "src", "rcv"), P(("grp", "src"), "rcv", None))
    out_specs = P("grp", None, "src", "rcv")
    return jax.shard_map(shards, mesh=mesh, in_specs=in_specs, out_specs=out_specs, check_vma=False)
```

```python
import functools

import jax
import jax.numpy as jnp
from jax import lax
from jax.experimental import pallas as pl
from jax.experimental.pallas import tpu as pltpu
from jax.sharding import PartitionSpec as P

NB = 32
TILE = 128
SIDE = 4
ROWS = 256
COLS = 512
X_LINES = [[SIDE * y + x for x in range(SIDE)] for y in range(SIDE)]
Y_LINES = [[SIDE * y + x for y in range(SIDE)] for x in range(SIDE)]


def tile_weights(aperture):
    block_ids = jnp.arange(NB, dtype=jnp.int32)
    offset = block_ids[None, None, :] - aperture[..., 0:1]
    extent = aperture[..., 1:2]
    taper_width = aperture[..., 2:3]
    margin = jnp.minimum(offset, extent - 1 - offset)
    ramped = jnp.minimum(
        1.0, (margin + 1).astype(jnp.float32) / (taper_width + 1).astype(jnp.float32)
    )
    return jnp.where((offset >= 0) & (offset < extent), ramped, 0.0)


def shift(block, dy, dx):
    pairs = [
        (SIDE * y + x, SIDE * ((y + dy) % SIDE) + (x + dx) % SIDE)
        for y in range(SIDE)
        for x in range(SIDE)
    ]
    return lax.ppermute(block, "src", pairs)


def along(block, lines):
    copies = jnp.broadcast_to(block, (SIDE, *block.shape[1:]))
    return lax.all_to_all(copies, "src", 0, 0, tiled=True, axis_index_groups=lines)


def locate(source, steps):
    y, x = source[0] // SIDE, lax.rem(source[0], SIDE)
    found = []
    for _, index, dy, dx in steps:
        row, column = lax.rem(y + dy, SIDE), lax.rem(x + dx, SIDE)
        found.append((row * SIDE + column, {"y": row, "x": column}.get(index, index)))
    return found


def sum_tile(weights, tile, places, lefts, rights):
    cols = slice(tile * TILE, (tile + 1) * TILE)
    total = None
    for place, left, right in zip(places, lefts, rights):
        parts = []
        for half in range(ROWS // TILE):
            lanes = slice(half * TILE, (half + 1) * TILE)
            rows = []
            for part in range(2):
                for a in range(2):
                    value = left[part, a * TILE : (a + 1) * TILE, lanes]
                    weight = weights[a * 4 + tile, 2 * place + half]
                    rows.append((value.astype(jnp.float32) * weight).astype(jnp.bfloat16))
            parts.append(jnp.concatenate(rows, axis=0))
        scaled = jnp.concatenate(parts, axis=1)
        both = jnp.concatenate([right[0, :, cols], right[1, :, cols]], axis=1)
        product = jnp.dot(scaled, both, preferred_element_type=jnp.float32)
        total = product if total is None else total + product
    real = total[:ROWS, :TILE] - total[ROWS:, TILE:]
    imag = total[:ROWS, TILE:] + total[ROWS:, :TILE]
    return cols, real, imag


def sum_early(steps, late, group, weights, source, left, *refs):
    *arrays, out, late_left, lefts, rights, left_done, right_done, late_done = refs

    def columns(place):
        return left.at[0, :, :, pl.ds(pl.multiple_of(place * ROWS, ROWS), ROWS)]

    places, copies = [], []
    for number, (place, index) in enumerate(locate(source, steps)):
        block = arrays[steps[number][0]].at[index]
        pair = (
            pltpu.make_async_copy(columns(place), lefts.at[number], left_done.at[number]),
            pltpu.make_async_copy(block, rights.at[number], right_done.at[number]),
        )
        for copy in pair:
            copy.start()
        places.append(place)
        copies.append(pair)
    kept = [
        pltpu.make_async_copy(columns(place), late_left.at[number], late_done.at[number])
        for number, (place, _) in enumerate(locate(source, late))
    ]
    for copy in kept:
        copy.start()
    for first in range(0, len(steps), group):
        numbers = range(first, min(first + group, len(steps)))
        for number in numbers:
            for copy in copies[number]:
                copy.wait()
        for tile in range(COLS // TILE):
            cols, real, imag = sum_tile(
                weights,
                tile,
                [places[n] for n in numbers],
                [lefts.at[n] for n in numbers],
                [rights.at[n] for n in numbers],
            )
            if first > 0:
                real, imag = real + out[0, 0, :, cols], imag + out[0, 1, :, cols]
            out[0, 0, :, cols] = real
            out[0, 1, :, cols] = imag
    for copy in kept:
        copy.wait()


def sum_late(steps, group, weights, source, base, late_left, *refs):
    *arrays, out, total, partial, lefts, rights, left_done, right_done, base_done, out_done = refs
    places, copies = [], []
    for number, (place, index) in enumerate(locate(source, steps)):
        block = arrays[steps[number][0]].at[index]
        pair = (
            pltpu.make_async_copy(late_left.at[number], lefts.at[number], left_done.at[number]),
            pltpu.make_async_copy(block, rights.at[number], right_done.at[number]),
        )
        for copy in pair:
            copy.start()
        places.append(place)
        copies.append(pair)
    fetch = pltpu.make_async_copy(base, total, base_done)
    fetch.start()
    stores = []
    for first in range(0, len(steps), group):
        numbers = range(first, min(first + group, len(steps)))
        for number in numbers:
            for copy in copies[number]:
                copy.wait()
        last = first + group >= len(steps)
        for tile in range(COLS // TILE):
            cols, real, imag = sum_tile(
                weights,
                tile,
                [places[n] for n in numbers],
                [lefts.at[n] for n in numbers],
                [rights.at[n] for n in numbers],
            )
            if last and first > 0 and tile == 0:
                fetch.wait()
            if first > 0:
                real, imag = real + partial[0, :, cols], imag + partial[1, :, cols]
            if last:
                total[0, 0, :, cols] += real
                total[0, 1, :, cols] += imag
            else:
                partial[0, :, cols] = real
                partial[1, :, cols] = imag
            if last:
                store = pltpu.make_async_copy(
                    total.at[0, :, :, cols], out.at[0, :, :, cols], out_done.at[tile]
                )
                store.start()
                stores.append(store)
    for store in stores:
        store.wait()


def cost(count, scale):
    return pl.CostEstimate(
        flops=count * 8 * scale * ROWS * ROWS * COLS,
        bytes_accessed=count * 3 * (1 << 18) + (2 << 20),
        transcendentals=0,
    )


SMEM = pl.BlockSpec(memory_space=pltpu.SMEM)
VMEM = pl.BlockSpec(memory_space=pltpu.VMEM)
HBM = pl.BlockSpec(memory_space=pltpu.HBM)
SUM = jax.ShapeDtypeStruct((1, 2, ROWS, COLS), jnp.float32)


def add_early(weights, source, left, arrays, steps, late):
    count = len(steps)
    return pl.pallas_call(
        functools.partial(sum_early, steps, late, 6),
        out_shape=(SUM, jax.ShapeDtypeStruct((len(late), 2, ROWS, ROWS), jnp.bfloat16)),
        in_specs=[SMEM, SMEM, HBM] + [HBM] * len(arrays),
        out_specs=(VMEM, VMEM),
        scratch_shapes=[
            pltpu.VMEM((count, 2, ROWS, ROWS), jnp.bfloat16),
            pltpu.VMEM((count, 2, ROWS, COLS), jnp.bfloat16),
            pltpu.SemaphoreType.DMA((count,)),
            pltpu.SemaphoreType.DMA((count,)),
            pltpu.SemaphoreType.DMA((len(late),)),
        ],
        compiler_params=pltpu.CompilerParams(vmem_limit_bytes=63 << 20),
        cost_estimate=cost(count, 3),
    )(weights, source, left, *arrays)


def add_late(weights, source, base, late_left, arrays, steps):
    count = len(steps)
    return pl.pallas_call(
        functools.partial(sum_late, steps, 2),
        out_shape=SUM,
        in_specs=[SMEM, SMEM, HBM, HBM] + [HBM] * len(arrays),
        out_specs=HBM,
        scratch_shapes=[
            pltpu.VMEM((1, 2, ROWS, COLS), jnp.float32),
            pltpu.VMEM((2, ROWS, COLS), jnp.float32),
            pltpu.VMEM((count, 2, ROWS, ROWS), jnp.bfloat16),
            pltpu.VMEM((count, 2, ROWS, COLS), jnp.bfloat16),
            pltpu.SemaphoreType.DMA((count,)),
            pltpu.SemaphoreType.DMA((count,)),
            pltpu.SemaphoreType.DMA,
            pltpu.SemaphoreType.DMA((COLS // TILE,)),
        ],
        compiler_params=pltpu.CompilerParams(vmem_limit_bytes=60 << 20),
        cost_estimate=cost(count, 3),
    )(weights, source, base, late_left, *arrays)


def place_both(first, second, out, done):
    copies = [
        pltpu.make_async_copy(block.at[0], out.at[n], done.at[n])
        for n, block in enumerate((first, second))
    ]
    for copy in copies:
        copy.start()
    for copy in copies:
        copy.wait()


def join(first, second):
    return pl.pallas_call(
        place_both,
        out_shape=jax.ShapeDtypeStruct((2, 2, ROWS, COLS), jnp.bfloat16),
        in_specs=[pl.BlockSpec(memory_space=pl.ANY)] * 2,
        out_specs=pl.BlockSpec(memory_space=pl.ANY),
        scratch_shapes=[pltpu.SemaphoreType.DMA((2,))],
        cost_estimate=pl.CostEstimate(flops=0, bytes_accessed=1 << 21, transcendentals=0),
    )(first, second)


def shards(recorded, aperture):
    weights = tile_weights(aperture).reshape(8, NB)
    source = lax.axis_index("src")
    x = source % SIDE
    y = source // SIDE
    left = lax.all_gather(recorded, "rcv", axis=3, tiled=True)
    above, below = shift(recorded, 1, 0), shift(recorded, -1, 0)
    before, after = shift(recorded, 0, 1), shift(recorded, 0, -1)
    opposite = shift(recorded, 0, 2)
    across = [shift(above[:, :1], 1, 0), shift(below[:, 1:], -1, 0)]
    *across, before, after, opposite, weights = lax.optimization_barrier(
        (*across, before, after, opposite, weights)
    )
    pair = join(above, below)
    pair_left, pair_right = shift(pair, 0, 1), shift(pair, 0, -1)
    far = jnp.concatenate(across, axis=1)
    across_line = along(far, X_LINES)
    opposite_above, opposite_below = shift(opposite, 1, 0), shift(opposite, -1, 0)

    early = [recorded, above, below, before, after, opposite, pair_left, pair_right, far]
    steps = [(0, 0, 0, 0), (1, 0, 3, 0), (2, 0, 1, 0), (3, 0, 0, 3), (4, 0, 0, 1), (5, 0, 0, 2)]
    steps += [(6, 0, 3, 3), (6, 1, 1, 3), (7, 0, 3, 1), (7, 1, 1, 1)]
    steps += [(8, 0, 2, 0)]
    late = [opposite_above, opposite_below, across_line]
    late_steps = [(0, 0, 3, 2), (1, 0, 1, 2)] + [(2, "x", 2, i) for i in range(1, SIDE)]
    source = source.reshape(1)
    total, late_left = add_early(weights, source, left, early, steps, late_steps)
    return add_late(weights, source, total, late_left, late, late_steps)


def solution(mesh):
    in_specs = (P("grp", None, "src", "rcv"), P(("grp", "src"), "rcv", None))
    out_specs = P("grp", None, "src", "rcv")
    return jax.shard_map(shards, mesh=mesh, in_specs=in_specs, out_specs=out_specs, check_vma=False)
```
